32 devices in a mesh: ens: 2 (over x), lat: 16 (over z, y, core).
Axes of the slice: x: 2, y: 2, z: 4, core: 2. Of those that a mesh axis runs over, the one named last changes fastest.
Arguments:
- spectral_in: bfloat16 [640, 2, 2, 64, 320], P('lat', None, None, 'ens'), parts along dimension 3, may hold values from -12 to 12
- legendre: bfloat16 [640, 2, 320, 640], P('lat'), may hold values from -0.25 to 0.25
- wave_of_slot: int32 [640], replicated, may hold values from 0 to 639, each once
Outputs:
- spectral_out: float32 [640, 2, 2, 64, 320], P('lat', None, None, 'ens'), parts along dimension 3
The draws below stay inside these ranges and needn't reach their ends.
There are 2 independent parts, one for each index of `ens`. The reference program is written for one: setup_inputs(seed, part) draws one part's arguments, and reference() takes and returns one part's arrays. A program takes and returns all parts, laid end to end along the dimension named above; an argument that names none is the same for every part. Nothing has to cross between parts.
Inputs may be any that keep to these rules, and one draw needn't show every extreme that they name: `wave_of_slot`: every wavenumber 0 to 639 stands in exactly one slot.
All inputs are finite; a program needn't handle non-finite values.
Results may differ from the reference program's by a relative error of at most 0.0073.
Values may be sent and summed in bfloat16 or wider, within the bound.
No kernel may reach another device: no remote copies, remote signals or barrier semaphores. Data moves between devices by JAX's collectives and lax.ppermute only.
A program may use at most 192 MiB of HBM per device.

```python
import math
import jax
import jax.numpy as jnp

NLON = 2560
NLAT = 1280
M = 640
FIELDS = 4
LEV = 8
S = 32
KH = 320
LATH = 640


def block_levels(key, dims, split, low, largest):
    factor_of, own = 1.0, jax.random.fold_in(key, 6)
    for dim, shards_of in split:
        draws = jnp.exp(jax.random.uniform(jax.random.fold_in(own, dim), (shards_of,), jnp.float32, low / len(split), largest / len(split)))
        factor_of = factor_of * jnp.repeat(draws, dims[dim] // shards_of).reshape([-1 if axis == dim else 1 for axis in range(len(dims))])
    return factor_of


def bell_draw(key, shape, width, most, shards=(), held_as=jnp.bfloat16):
    array = jax.random.normal(key, shape, jnp.float32) * width
    if len(shards) > 0:
        array = block_levels(key, shape, shards, -0.22, 0.18) * array
    return jnp.clip(array, min=-most, max=most).astype(held_as)


def setup_inputs(seed: int = 0, part: int = 0) -> dict:
    seeds = jax.random.split(jax.random.key(seed), 4)
    part_keys = jax.random.split(jax.random.fold_in(seeds[3], part), 4)
    return {
        "spectral_in": bell_draw(part_keys[0], (M, 2, 2, S, KH), 2.0, 12.0, ((0, 16),)),
        "legendre": bell_draw(seeds[1], (M, 2, KH, LATH), LATH ** -0.5, 0.25, ((0, 16),)),
        "wave_of_slot": jax.random.permutation(seeds[2], M).astype(jnp.int32),
    }


def validity(wavenumbers, total, half):
    ranks = 2 * jnp.arange(half, dtype=jnp.int32)[None, :] + jnp.arange(2, dtype=jnp.int32)[:, None]
    return ranks[None, :, :] <= (total - 1 - wavenumbers.astype(jnp.int32))[:, None, None]

def basis_tables(wave_of_slot):
    wavenumbers = wave_of_slot.astype(jnp.int32)
    longitudes = jnp.arange(NLON, dtype=jnp.int32)
    phases = wavenumbers[:, None] * longitudes[None, :] % NLON
    angles = phases.astype(jnp.float32) * (2.0 * math.pi / NLON)
    factor = 1.0 / math.sqrt(NLON)
    cosine = jnp.cos(angles) * factor
    sine_part = jnp.sin(angles) * factor
    weights = jnp.where(wavenumbers == 0, 1.0, 2.0).astype(jnp.float32)[:, None]
    synthesis = jnp.stack([weights * cosine, -weights * sine_part]).astype(jnp.bfloat16)
    analysis = jnp.stack([cosine, -sine_part]).astype(jnp.bfloat16)
    return (synthesis, analysis)

def reference(spectral_in, legendre, wave_of_slot):
    is_valid = validity(wave_of_slot, M, KH)
    masked = jnp.where(is_valid[:, :, None, None, :], spectral_in, jnp.zeros_like(spectral_in))
    legendre_wide = legendre.astype(jnp.float32)
    parity_sum = jnp.einsum('sprj,spclr->spclj', legendre_wide, masked.astype(jnp.float32))
    north_rows = parity_sum[:, 0] + parity_sum[:, 1]
    south_rows = (parity_sum[:, 0] - parity_sum[:, 1])[..., ::-1]
    fourier = jnp.concatenate([north_rows, south_rows], axis=3).astype(jnp.bfloat16)
    synthesis, analysis = basis_tables(wave_of_slot)
    grid_field = jnp.einsum('scli,csx->lix', fourier.astype(jnp.float32), synthesis.astype(jnp.float32))
    partner = jnp.roll(grid_field.reshape(FIELDS, LEV, NLAT, NLON), -1, axis=0).reshape(grid_field.shape)
    product = (grid_field * partner).astype(jnp.bfloat16)
    coefficients = jnp.einsum('lix,csx->csli', product.astype(jnp.float32), analysis.astype(jnp.float32)).astype(jnp.bfloat16)
    north_part = coefficients[..., :LATH].astype(jnp.float32)
    south_part = coefficients[..., LATH:][..., ::-1].astype(jnp.float32)
    folded = jnp.stack([north_part + south_part, north_part - south_part]).astype(jnp.bfloat16)
    result = jnp.einsum('sprj,pcslj->spclr', legendre_wide, folded.astype(jnp.float32))
    return jnp.where(is_valid[:, :, None, None, :], result, jnp.zeros_like(result))
```

```python
import math

import jax
import jax.numpy as jnp
from jax import lax
from jax.experimental import pallas as pl
from jax.experimental.pallas import tpu as pltpu
from jax.sharding import PartitionSpec as P

NLON = 2560
FIELDS = 4
HALF = NLON // 2
LANES = 128
SLOTS_PER_STEP = 8
XBLOCK = 256
SBLOCK = 128
VMEM = 56 << 20


def quarter_sine(t):
    u = t * t
    p = jnp.float32(-3.5988432e-6)
    for coefficient in (1.60441184787e-4, -4.68175413532e-3, 7.96926262462e-2, -6.45964097506e-1, 1.57079632679):
        p = p * u + jnp.float32(coefficient)
    return p * t


def phase_turn(waves, points):
    product = waves * points
    return product - NLON * jnp.round(product * (1.0 / NLON))


def cosine_of(turn):
    return quarter_sine((HALF // 2 - jnp.abs(turn)) * (2.0 / HALF))


def sine_of(turn):
    size = jnp.abs(turn)
    return jnp.sign(turn) * quarter_sine(jnp.minimum(size, HALF - size) * (2.0 / HALF))


def half_tables(waves):
    m = waves.astype(jnp.float32)
    factor = 1.0 / math.sqrt(NLON)
    weight = jnp.where(waves == 0, 1.0, 2.0).astype(jnp.float32)
    x = jnp.arange(HALF + 16, dtype=jnp.float32)
    turn = phase_turn(m[None, :], x[:, None])
    synthesis_cos = (cosine_of(turn) * factor * weight[None, :]).astype(jnp.bfloat16)
    synthesis_sin = (-sine_of(turn[:HALF]) * factor * weight[None, :]).astype(jnp.bfloat16)
    x = x[:HALF]
    twice = jnp.where(x == 0, 1.0, 2.0)[None, :]
    turn = phase_turn(m[:, None], x[None, :])
    analysis_cos = (cosine_of(turn) * factor * twice).astype(jnp.bfloat16)
    analysis_sin = (-sine_of(turn) * factor * twice).astype(jnp.bfloat16)
    alternate = jnp.where(waves % 2 == 0, factor, -factor).astype(jnp.bfloat16).astype(jnp.float32)
    return synthesis_cos, synthesis_sin, analysis_cos, analysis_sin, alternate[:, None]


def synthesis_kernel(count_ref, spectral_ref, legendre_ref, out_ref, scratch):
    step = pl.program_id(0)
    levels = out_ref.shape[0] // 2
    rows = spectral_ref.shape[2] * spectral_ref.shape[3]
    half = spectral_ref.shape[4]
    lane = lax.broadcasted_iota(jnp.int32, (rows, half), 1)
    for s in range(SLOTS_PER_STEP):
        parts = []
        for p in range(2):
            values = spectral_ref[s, p].reshape(rows, half).astype(jnp.float32)
            count = count_ref[step * SLOTS_PER_STEP + s, p]
            values = jnp.where(lane < count, values, 0.0).astype(jnp.bfloat16)
            parts.append(jnp.dot(values, legendre_ref[s, p], preferred_element_type=jnp.float32))
        scratch[s, 0] = parts[0] + parts[1]
        scratch[s, 1] = parts[0] - parts[1]
        for v in range(levels):
            for ns in range(2):
                tile = scratch[s, ns, pl.ds(v, rows // levels, stride=levels), :]
                out_ref[2 * v + ns, s] = tile.astype(jnp.bfloat16)


def synthesize(counts, spectral, legendre, chunk):
    slots, _, _, slabs, half = spectral.shape
    levels = slabs // FIELDS
    rows = 2 * FIELDS
    return pl.pallas_call(
        synthesis_kernel,
        grid_spec=pltpu.PrefetchScalarGridSpec(
            num_scalar_prefetch=1,
            grid=(slots // SLOTS_PER_STEP,),
            in_specs=[
                pl.BlockSpec((SLOTS_PER_STEP, 2, 2, slabs, half), lambda i, c: (i, 0, 0, 0, 0)),
                pl.BlockSpec((SLOTS_PER_STEP, 2, half, LANES), lambda i, c: (i, 0, 0, chunk)),
            ],
            out_specs=pl.BlockSpec((2 * levels, SLOTS_PER_STEP, rows, LANES), lambda i, c: (0, i, 0, 0)),
            scratch_shapes=[pltpu.VMEM((SLOTS_PER_STEP, 2, 2 * slabs, LANES), jnp.float32)],
        ),
        out_shape=jax.ShapeDtypeStruct((2 * levels, slots, rows, LANES), jnp.bfloat16),
        compiler_params=pltpu.CompilerParams(vmem_limit_bytes=VMEM),
        cost_estimate=pl.CostEstimate(
            flops=2 * slots * 2 * 2 * slabs * half * LANES,
            transcendentals=0,
            bytes_accessed=slots * 2 * half * (LANES + 2 * slabs) * 2,
        ),
        name="legendre_synthesis",
    )(counts, spectral, legendre)


def grid_kernel(y_ref, sc_ref, ss_ref, ac_ref, as_ref, alt_ref, out_ref, wide, cos_in, sin_in, even, odd):
    waves = y_ref.shape[0]
    rows = y_ref.shape[1]
    width = FIELDS * LANES
    wide[...] = y_ref[...].reshape(waves * rows, LANES).astype(jnp.float32)
    for f in range(FIELDS):
        columns = pl.ds(f * LANES, LANES)
        cos_in[:, columns] = wide[pl.ds(f, waves, stride=rows), :].astype(jnp.bfloat16)
        sin_in[:, columns] = wide[pl.ds(FIELDS + f, waves, stride=rows), :].astype(jnp.bfloat16)

    def partner(a):
        return jnp.concatenate([a[:, LANES:], a[:, :LANES]], axis=1)

    for b in range(HALF // XBLOCK):
        points = pl.ds(b * XBLOCK, XBLOCK)
        e = jnp.dot(sc_ref[points, :], cos_in[...], preferred_element_type=jnp.float32)
        o = jnp.dot(ss_ref[points, :], sin_in[...], preferred_element_type=jnp.float32)
        e2, o2 = partner(e), partner(o)
        even[points, :] = (e * e2 + o * o2).astype(jnp.bfloat16)
        odd[points, :] = (e * o2 + o * e2).astype(jnp.bfloat16)
    middle = jnp.dot(sc_ref[pl.ds(HALF, 16), :], cos_in[...], preferred_element_type=jnp.float32)
    middle = (middle * partner(middle)).astype(jnp.bfloat16).astype(jnp.float32)[0:1, :]

    for b in range(waves // SBLOCK):
        slots = pl.ds(b * SBLOCK, SBLOCK)
        cos_out = jnp.dot(ac_ref[slots, :], even[...], preferred_element_type=jnp.float32)
        cos_out = cos_out + alt_ref[slots, :] * middle
        sin_out = jnp.dot(as_ref[slots, :], odd[...], preferred_element_type=jnp.float32)
        for f in range(FIELDS):
            columns = slice(f * LANES, (f + 1) * LANES)
            wide[pl.ds(b * SBLOCK * rows + f, SBLOCK, stride=rows), :] = cos_out[:, columns]
            wide[pl.ds(b * SBLOCK * rows + FIELDS + f, SBLOCK, stride=rows), :] = sin_out[:, columns]
    out_ref[...] = wide[...].astype(jnp.bfloat16).reshape(waves, rows, LANES)


def grid_product(y, tables):
    waves, rows, _ = y.shape
    width = FIELDS * LANES
    return pl.pallas_call(
        grid_kernel,
        out_shape=jax.ShapeDtypeStruct(y.shape, jnp.bfloat16),
        scratch_shapes=[
            pltpu.VMEM((waves * rows, LANES), jnp.float32),
            pltpu.VMEM((waves, width), jnp.bfloat16),
            pltpu.VMEM((waves, width), jnp.bfloat16),
            pltpu.VMEM((HALF, width), jnp.bfloat16),
            pltpu.VMEM((HALF, width), jnp.bfloat16),
        ],
        compiler_params=pltpu.CompilerParams(vmem_limit_bytes=VMEM),
        cost_estimate=pl.CostEstimate(
            flops=8 * waves * HALF * width, transcendentals=0, bytes_accessed=8 * waves * HALF + 4 * waves * rows * LANES
        ),
        name="grid_product",
    )(y, *tables)


def projection_kernel(chunks, added, count_ref, *refs):
    arrived = refs[:chunks]
    legendres = refs[chunks : 2 * chunks]
    before = refs[2 * chunks] if added else None
    out_ref, scratch = refs[-2], refs[-1]
    step = pl.program_id(0)
    levels = arrived[0].shape[0] // 2
    fields = arrived[0].shape[2]
    rows = levels * fields
    half = legendres[0].shape[2]
    lane = lax.broadcasted_iota(jnp.int32, (rows, half), 1)
    for s in range(SLOTS_PER_STEP):
        sums = [None, None]
        for k in range(chunks):
            for v in range(levels):
                north = arrived[k][2 * v, s].astype(jnp.float32)
                south = arrived[k][2 * v + 1, s].astype(jnp.float32)
                scratch[s, k, 0, pl.ds(v * fields, fields), :] = north + south
                scratch[s, k, 1, pl.ds(v * fields, fields), :] = north - south
            for p in range(2):
                folded = jnp.concatenate(
                    [scratch[s, k, p, pl.ds(r, levels, stride=fields), :] for r in range(fields)], axis=0
                ).astype(jnp.bfloat16)
                part = lax.dot_general(
                    folded, legendres[k][s, p], (((1,), (1,)), ((), ())), preferred_element_type=jnp.float32
                )
                sums[p] = part if sums[p] is None else sums[p] + part
        for p in range(2):
            count = count_ref[step * SLOTS_PER_STEP + s, p]
            value = jnp.where(lane < count, sums[p], 0.0).reshape(out_ref.shape[2:])
            if added:
                value = value + before[s, p]
            out_ref[s, p] = value


def project(counts, arrived, legendre, chunk_ids, before=None):
    chunks = len(arrived)
    ranks, slots, fields, _ = arrived[0].shape
    slabs = ranks // 2 * FIELDS
    half = legendre.shape[2]
    n = SLOTS_PER_STEP
    out_spec = pl.BlockSpec((n, 2, 2, slabs, half), lambda i, c: (i, 0, 0, 0, 0))
    added = before is not None

    def kernel(*refs):
        projection_kernel(chunks, added, *refs)

    return pl.pallas_call(
        kernel,
        grid_spec=pltpu.PrefetchScalarGridSpec(
            num_scalar_prefetch=1,
            grid=(slots // n,),
            in_specs=[pl.BlockSpec((ranks, n, fields, LANES), lambda i, c: (0, i, 0, 0))] * chunks
            + [pl.BlockSpec((n, 2, half, LANES), lambda i, c, k=k: (i, 0, 0, k)) for k in chunk_ids]
            + ([out_spec] if added else []),
            out_specs=out_spec,
            scratch_shapes=[pltpu.VMEM((n, chunks, 2, 2 * slabs, LANES), jnp.float32)],
        ),
        out_shape=jax.ShapeDtypeStruct((slots, 2, 2, slabs, half), jnp.float32),
        input_output_aliases={1 + 2 * chunks: 0} if added else {},
        compiler_params=pltpu.CompilerParams(vmem_limit_bytes=VMEM),
        cost_estimate=pl.CostEstimate(
            flops=2 * chunks * slots * 2 * 2 * slabs * half * LANES,
            transcendentals=0,
            bytes_accessed=slots * 2 * half * (chunks * LANES + 4 * slabs) * 2,
        ),
        name="legendre_projection",
    )(counts, *arrived, *([legendre] * chunks), *([before] if added else []))


def per_device(spectral_in, legendre, wave_of_slot):
    slots, _, _, slabs, half = spectral_in.shape
    total = wave_of_slot.shape[0]
    ranks = total // slots
    chunks = legendre.shape[3] // LANES
    start = lax.axis_index("lat") * slots
    own = lax.dynamic_slice_in_dim(wave_of_slot, start, slots)
    counts = (total + 1 - own[:, None] - jnp.arange(2, dtype=jnp.int32)[None, :]) // 2
    tables = half_tables(wave_of_slot)

    def exchange(x):
        return lax.all_to_all(x, "lat", split_axis=0, concat_axis=0, tiled=True)

    sent = [exchange(synthesize(counts, spectral_in, legendre, k)) for k in range(chunks)]
    back = []
    for y in sent:
        product = grid_product(y.reshape(total, 2 * FIELDS, LANES), tables)
        back.append(exchange(product.reshape(ranks, slots, 2 * FIELDS, LANES)))
    first = project(counts, back[:-1], legendre, range(chunks - 1))
    return project(counts, back[-1:], legendre, [chunks - 1], first)


def basis_tables(wave_of_slot):
    longitudes = jnp.arange(NLON, dtype=jnp.int32)
    phases = wave_of_slot[:, None] * longitudes[None, :] % NLON
    angles = phases.astype(jnp.float32) * (2.0 * math.pi / NLON)
    factor = 1.0 / math.sqrt(NLON)
    cosine = jnp.cos(angles) * factor
    sine_part = jnp.sin(angles) * factor
    weights = jnp.where(wave_of_slot == 0, 1.0, 2.0).astype(jnp.float32)[:, None]
    synthesis = jnp.stack([weights * cosine, -weights * sine_part]).astype(jnp.bfloat16)
    analysis = jnp.stack([cosine, -sine_part]).astype(jnp.bfloat16)
    return synthesis, analysis


def per_device_general(spectral_in, legendre, wave_of_slot):
    slot_count, _, half, north = legendre.shape
    total = wave_of_slot.shape[0]
    own = lax.dynamic_slice_in_dim(wave_of_slot, lax.axis_index("lat") * slot_count, slot_count)
    ranks = 2 * jnp.arange(half, dtype=jnp.int32)[None, :] + jnp.arange(2, dtype=jnp.int32)[:, None]
    is_valid = (ranks[None] <= (total - 1 - own)[:, None, None])[:, :, None, None, :]
    masked = jnp.where(is_valid, spectral_in, jnp.zeros_like(spectral_in))
    sums = jnp.einsum("sprj,spclr->spclj", legendre, masked, preferred_element_type=jnp.float32)
    south = (sums[:, 0] - sums[:, 1])[..., ::-1]
    fourier = jnp.concatenate([sums[:, 0] + sums[:, 1], south], axis=3).astype(jnp.bfloat16)
    spread = lax.all_to_all(fourier, "lat", split_axis=3, concat_axis=0, tiled=True)
    synthesis, analysis = basis_tables(wave_of_slot)
    field = jnp.einsum("scli,csx->lix", spread, synthesis, preferred_element_type=jnp.float32)
    levels = field.shape[0] // FIELDS
    partner = jnp.roll(field.reshape((FIELDS, levels) + field.shape[1:]), -1, axis=0).reshape(field.shape)
    product = (field * partner).astype(jnp.bfloat16)
    coefficients = jnp.einsum("lix,csx->csli", product, analysis, preferred_element_type=jnp.float32)
    gathered = lax.all_to_all(coefficients.astype(jnp.bfloat16), "lat", split_axis=1, concat_axis=3, tiled=True)
    north_part = gathered[..., :north].astype(jnp.float32)
    south_part = gathered[..., north:][..., ::-1].astype(jnp.float32)
    folded = jnp.stack([north_part + south_part, north_part - south_part]).astype(jnp.bfloat16)
    result = jnp.einsum("sprj,pcslj->spclr", legendre, folded, preferred_element_type=jnp.float32)
    return jnp.where(is_valid, result, jnp.zeros_like(result))


def solution(mesh):
    rows = mesh.shape["lat"]

    def local(spectral_in, legendre, wave_of_slot):
        slots, _, _, slabs, _ = spectral_in.shape
        whole_tiles = slots % SLOTS_PER_STEP == 0 and legendre.shape[3] % LANES == 0
        if rows * FIELDS == 2 * slabs and whole_tiles and wave_of_slot.shape[0] % SBLOCK == 0:
            return per_device(spectral_in, legendre, wave_of_slot)
        return per_device_general(spectral_in, legendre, wave_of_slot)

    return jax.shard_map(
        local,
        mesh=mesh,
        in_specs=(P("lat", None, None, "ens", None), P("lat", None, None, None), P()),
        out_specs=P("lat", None, None, "ens", None),
        check_vma=False,
    )
```

```python
import math

import jax
import jax.numpy as jnp
from jax import lax
from jax.experimental import pallas as pl
from jax.experimental.pallas import tpu as pltpu
from jax.sharding import PartitionSpec as P

NLON = 2560
FIELDS = 4
HALF = NLON // 2
LANES = 128
SLOTS_PER_STEP = 8
XBLOCK = 256
SBLOCK = 128
VMEM = 56 << 20
FORWARD = (1, 4)
RETURN = ((0, 0, 1), (1, 0, 3), (1, 3, 1))


def quarter_sine(t):
    u = t * t
    p = jnp.float32(-3.5988432e-6)
    for coefficient in (1.60441184787e-4, -4.68175413532e-3, 7.96926262462e-2, -6.45964097506e-1, 1.57079632679):
        p = p * u + jnp.float32(coefficient)
    return p * t


def phase_turn(waves, points):
    product = waves * points
    return product - NLON * jnp.round(product * (1.0 / NLON))


def cosine_of(turn):
    return quarter_sine((HALF // 2 - jnp.abs(turn)) * (2.0 / HALF))


def sine_of(turn):
    size = jnp.abs(turn)
    return jnp.sign(turn) * quarter_sine(jnp.minimum(size, HALF - size) * (2.0 / HALF))


def half_tables(waves):
    m = waves.astype(jnp.float32)
    factor = 1.0 / math.sqrt(NLON)
    weight = jnp.where(waves == 0, 1.0, 2.0).astype(jnp.float32)
    x = jnp.arange(HALF + 16, dtype=jnp.float32)
    turn = phase_turn(m[None, :], x[:, None])
    synthesis_cos = (cosine_of(turn) * factor * weight[None, :]).astype(jnp.bfloat16)
    synthesis_sin = (-sine_of(turn[:HALF]) * factor * weight[None, :]).astype(jnp.bfloat16)
    x = x[:HALF]
    twice = jnp.where(x == 0, 1.0, 2.0)[None, :]
    turn = phase_turn(m[:, None], x[None, :])
    analysis_cos = (cosine_of(turn) * factor * twice).astype(jnp.bfloat16)
    analysis_sin = (-sine_of(turn) * factor * twice).astype(jnp.bfloat16)
    alternate = jnp.where(waves % 2 == 0, factor, -factor).astype(jnp.bfloat16).astype(jnp.float32)
    return synthesis_cos, synthesis_sin, analysis_cos, analysis_sin, alternate[:, None]


def synthesis_kernel(count_ref, spectral_ref, legendre_ref, out_ref, scratch):
    step = pl.program_id(1)
    levels = out_ref.shape[0] // 2
    rows = spectral_ref.shape[2] * spectral_ref.shape[3]
    half = spectral_ref.shape[4]
    lane = lax.broadcasted_iota(jnp.int32, (rows, half), 1)
    for s in range(SLOTS_PER_STEP):
        parts = []
        for p in range(2):
            values = spectral_ref[s, p].reshape(rows, half).astype(jnp.float32)
            count = count_ref[step * SLOTS_PER_STEP + s, p]
            values = jnp.where(lane < count, values, 0.0).astype(jnp.bfloat16)
            parts.append(jnp.dot(values, legendre_ref[s, p], preferred_element_type=jnp.float32))
        scratch[s, 0] = parts[0] + parts[1]
        scratch[s, 1] = parts[0] - parts[1]
        for v in range(levels):
            for ns in range(2):
                tile = scratch[s, ns, pl.ds(v, rows // levels, stride=levels), :]
                out_ref[2 * v + ns, 0, s] = tile.astype(jnp.bfloat16)


def synthesize(counts, spectral, legendre, units):
    slots, _, _, slabs, half = spectral.shape
    levels = slabs // FIELDS
    rows = 2 * FIELDS
    return pl.pallas_call(
        synthesis_kernel,
        grid_spec=pltpu.PrefetchScalarGridSpec(
            num_scalar_prefetch=1,
            grid=(len(units), slots // SLOTS_PER_STEP),
            in_specs=[
                pl.BlockSpec((SLOTS_PER_STEP, 2, 2, slabs, half), lambda u, i, c: (i, 0, 0, 0, 0)),
                pl.BlockSpec((SLOTS_PER_STEP, 2, half, LANES), lambda u, i, c: (i, 0, 0, units[0] + u)),
            ],
            out_specs=pl.BlockSpec((2 * levels, 1, SLOTS_PER_STEP, rows, LANES), lambda u, i, c: (0, u, i, 0, 0)),
            scratch_shapes=[pltpu.VMEM((SLOTS_PER_STEP, 2, 2 * slabs, LANES), jnp.float32)],
        ),
        out_shape=jax.ShapeDtypeStruct((2 * levels, len(units), slots, rows, LANES), jnp.bfloat16),
        compiler_params=pltpu.CompilerParams(vmem_limit_bytes=VMEM),
        cost_estimate=pl.CostEstimate(
            flops=2 * slots * 2 * 2 * slabs * half * LANES,
            transcendentals=0,
            bytes_accessed=slots * 2 * half * (LANES + 2 * slabs) * 2,
        ),
        name="legendre_synthesis",
    )(counts, spectral, legendre)


def grid_kernel(y_ref, sc_ref, ss_ref, ac_ref, as_ref, alt_ref, out_ref, wide, cos_in, sin_in, even, odd):
    ranks, _, slots, rows, _ = y_ref.shape
    waves = ranks * slots
    wide[...] = y_ref[...].reshape(waves * rows, LANES).astype(jnp.float32)
    for f in range(FIELDS):
        columns = pl.ds(f * LANES, LANES)
        cos_in[:, columns] = wide[pl.ds(f, waves, stride=rows), :].astype(jnp.bfloat16)
        sin_in[:, columns] = wide[pl.ds(FIELDS + f, waves, stride=rows), :].astype(jnp.bfloat16)

    def partner(a):
        return jnp.concatenate([a[:, LANES:], a[:, :LANES]], axis=1)

    for b in range(HALF // XBLOCK):
        points = pl.ds(b * XBLOCK, XBLOCK)
        e = jnp.dot(sc_ref[points, :], cos_in[...], preferred_element_type=jnp.float32)
        o = jnp.dot(ss_ref[points, :], sin_in[...], preferred_element_type=jnp.float32)
        e2, o2 = partner(e), partner(o)
        even[points, :] = (e * e2 + o * o2).astype(jnp.bfloat16)
        odd[points, :] = (e * o2 + o * e2).astype(jnp.bfloat16)
    middle = jnp.dot(sc_ref[pl.ds(HALF, 16), :], cos_in[...], preferred_element_type=jnp.float32)
    middle = (middle * partner(middle)).astype(jnp.bfloat16).astype(jnp.float32)[0:1, :]

    for b in range(waves // SBLOCK):
        part = pl.ds(b * SBLOCK, SBLOCK)
        cos_out = jnp.dot(ac_ref[part, :], even[...], preferred_element_type=jnp.float32)
        cos_out = cos_out + alt_ref[part, :] * middle
        sin_out = jnp.dot(as_ref[part, :], odd[...], preferred_element_type=jnp.float32)
        for f in range(FIELDS):
            columns = slice(f * LANES, (f + 1) * LANES)
            wide[pl.ds(b * SBLOCK * rows + f, SBLOCK, stride=rows), :] = cos_out[:, columns]
            wide[pl.ds(b * SBLOCK * rows + FIELDS + f, SBLOCK, stride=rows), :] = sin_out[:, columns]
    out_ref[...] = wide[...].astype(jnp.bfloat16).reshape(ranks, 1, slots, rows, LANES)


def grid_product(y, tables, first, units):
    ranks, _, slots, rows, _ = y.shape
    waves = ranks * slots
    width = FIELDS * LANES
    return pl.pallas_call(
        grid_kernel,
        grid=(units,),
        in_specs=[pl.BlockSpec((ranks, 1, slots, rows, LANES), lambda u: (0, first + u, 0, 0, 0))]
        + [pl.BlockSpec(t.shape, lambda u: (0, 0)) for t in tables],
        out_specs=pl.BlockSpec((ranks, 1, slots, rows, LANES), lambda u: (0, u, 0, 0, 0)),
        out_shape=jax.ShapeDtypeStruct((ranks, units, slots, rows, LANES), jnp.bfloat16),
        scratch_shapes=[
            pltpu.VMEM((waves * rows, LANES), jnp.float32),
            pltpu.VMEM((waves, width), jnp.bfloat16),
            pltpu.VMEM((waves, width), jnp.bfloat16),
            pltpu.VMEM((HALF, width), jnp.bfloat16),
            pltpu.VMEM((HALF, width), jnp.bfloat16),
        ],
        compiler_params=pltpu.CompilerParams(vmem_limit_bytes=VMEM),
        cost_estimate=pl.CostEstimate(
            flops=units * 8 * waves * HALF * width,
            transcendentals=0,
            bytes_accessed=8 * waves * HALF + units * 4 * waves * rows * LANES,
        ),
        name="grid_product",
    )(y, *tables)


def projection_kernel(sizes, added, count_ref, *refs):
    chunks = sum(sizes)
    arrived = refs[: len(sizes)]
    legendres = refs[len(sizes) : len(sizes) + chunks]
    before = refs[len(sizes) + chunks] if added else None
    homes = [(arrived[c], u) for c in range(len(sizes)) for u in range(sizes[c])]
    out_ref, scratch = refs[-2], refs[-1]
    step = pl.program_id(0)
    levels = arrived[0].shape[0] // 2
    fields = arrived[0].shape[3]
    rows = levels * fields
    half = legendres[0].shape[2]
    lane = lax.broadcasted_iota(jnp.int32, (rows, half), 1)
    for s in range(SLOTS_PER_STEP):
        sums = [None, None]
        for k in range(chunks):
            for v in range(levels):
                ref, u = homes[k]
                north = ref[2 * v, u, s].astype(jnp.float32)
                south = ref[2 * v + 1, u, s].astype(jnp.float32)
                scratch[s, k, 0, pl.ds(v * fields, fields), :] = north + south
                scratch[s, k, 1, pl.ds(v * fields, fields), :] = north - south
            for p in range(2):
                folded = jnp.concatenate(
                    [scratch[s, k, p, pl.ds(r, levels, stride=fields), :] for r in range(fields)], axis=0
                ).astype(jnp.bfloat16)
                part = lax.dot_general(
                    folded, legendres[k][s, p], (((1,), (1,)), ((), ())), preferred_element_type=jnp.float32
                )
                sums[p] = part if sums[p] is None else sums[p] + part
        for p in range(2):
            count = count_ref[step * SLOTS_PER_STEP + s, p]
            value = jnp.where(lane < count, sums[p], 0.0).reshape(out_ref.shape[2:])
            if added:
                value = value + before[s, p]
            out_ref[s, p] = value


def project(counts, arrived, legendre, chunk_ids, before=None):
    sizes = [a.shape[1] for a in arrived]
    chunks = len(chunk_ids)
    ranks, _, slots, fields, _ = arrived[0].shape
    slabs = ranks // 2 * FIELDS
    half = legendre.shape[2]
    n = SLOTS_PER_STEP
    out_spec = pl.BlockSpec((n, 2, 2, slabs, half), lambda i, c: (i, 0, 0, 0, 0))
    added = before is not None

    def kernel(*refs):
        projection_kernel(sizes, added, *refs)

    return pl.pallas_call(
        kernel,
        grid_spec=pltpu.PrefetchScalarGridSpec(
            num_scalar_prefetch=1,
            grid=(slots // n,),
            in_specs=[pl.BlockSpec((ranks, size, n, fields, LANES), lambda i, c: (0, 0, i, 0, 0)) for size in sizes]
            + [pl.BlockSpec((n, 2, half, LANES), lambda i, c, k=k: (i, 0, 0, k)) for k in chunk_ids]
            + ([out_spec] if added else []),
            out_specs=out_spec,
            scratch_shapes=[pltpu.VMEM((n, chunks, 2, 2 * slabs, LANES), jnp.float32)],
        ),
        out_shape=jax.ShapeDtypeStruct((slots, 2, 2, slabs, half), jnp.float32),
        input_output_aliases={1 + len(sizes) + chunks: 0} if added else {},
        compiler_params=pltpu.CompilerParams(vmem_limit_bytes=VMEM),
        cost_estimate=pl.CostEstimate(
            flops=2 * chunks * slots * 2 * 2 * slabs * half * LANES,
            transcendentals=0,
            bytes_accessed=slots * 2 * half * (chunks * LANES + 4 * slabs) * 2,
        ),
        name="legendre_projection",
    )(counts, *arrived, *([legendre] * chunks), *([before] if added else []))


def per_device(spectral_in, legendre, wave_of_slot):
    slots, _, _, slabs, half = spectral_in.shape
    total = wave_of_slot.shape[0]
    ranks = total // slots
    start = lax.axis_index("lat") * slots
    own = lax.dynamic_slice_in_dim(wave_of_slot, start, slots)
    counts = (total + 1 - own[:, None] - jnp.arange(2, dtype=jnp.int32)[None, :]) // 2
    tables = half_tables(wave_of_slot)

    def exchange(x):
        return lax.all_to_all(x, "lat", split_axis=0, concat_axis=0, tiled=True)

    sent, at = [], 0
    for size in FORWARD:
        sent.append(exchange(synthesize(counts, spectral_in, legendre, range(at, at + size))))
        at += size
    back = [exchange(grid_product(sent[c], tables, first, units)) for c, first, units in RETURN]
    places = [sum(FORWARD[:c]) + first for c, first, _ in RETURN]
    ids = [list(range(p, p + r[2])) for p, r in zip(places, RETURN)]
    sums = project(counts, back[:-1], legendre, [k for i in ids[:-1] for k in i])
    return project(counts, back[-1:], legendre, ids[-1], sums)


def basis_tables(wave_of_slot):
    longitudes = jnp.arange(NLON, dtype=jnp.int32)
    phases = wave_of_slot[:, None] * longitudes[None, :] % NLON
    angles = phases.astype(jnp.float32) * (2.0 * math.pi / NLON)
    factor = 1.0 / math.sqrt(NLON)
    cosine = jnp.cos(angles) * factor
    sine_part = jnp.sin(angles) * factor
    weights = jnp.where(wave_of_slot == 0, 1.0, 2.0).astype(jnp.float32)[:, None]
    synthesis = jnp.stack([weights * cosine, -weights * sine_part]).astype(jnp.bfloat16)
    analysis = jnp.stack([cosine, -sine_part]).astype(jnp.bfloat16)
    return synthesis, analysis


def per_device_general(spectral_in, legendre, wave_of_slot):
    slot_count, _, half, north = legendre.shape
    total = wave_of_slot.shape[0]
    own = lax.dynamic_slice_in_dim(wave_of_slot, lax.axis_index("lat") * slot_count, slot_count)
    ranks = 2 * jnp.arange(half, dtype=jnp.int32)[None, :] + jnp.arange(2, dtype=jnp.int32)[:, None]
    is_valid = (ranks[None] <= (total - 1 - own)[:, None, None])[:, :, None, None, :]
    masked = jnp.where(is_valid, spectral_in, jnp.zeros_like(spectral_in))
    sums = jnp.einsum("sprj,spclr->spclj", legendre, masked, preferred_element_type=jnp.float32)
    south = (sums[:, 0] - sums[:, 1])[..., ::-1]
    fourier = jnp.concatenate([sums[:, 0] + sums[:, 1], south], axis=3).astype(jnp.bfloat16)
    spread = lax.all_to_all(fourier, "lat", split_axis=3, concat_axis=0, tiled=True)
    synthesis, analysis = basis_tables(wave_of_slot)
    field = jnp.einsum("scli,csx->lix", spread, synthesis, preferred_element_type=jnp.float32)
    levels = field.shape[0] // FIELDS
    partner = jnp.roll(field.reshape((FIELDS, levels) + field.shape[1:]), -1, axis=0).reshape(field.shape)
    product = (field * partner).astype(jnp.bfloat16)
    coefficients = jnp.einsum("lix,csx->csli", product, analysis, preferred_element_type=jnp.float32)
    gathered = lax.all_to_all(coefficients.astype(jnp.bfloat16), "lat", split_axis=1, concat_axis=3, tiled=True)
    north_part = gathered[..., :north].astype(jnp.float32)
    south_part = gathered[..., north:][..., ::-1].astype(jnp.float32)
    folded = jnp.stack([north_part + south_part, north_part - south_part]).astype(jnp.bfloat16)
    result = jnp.einsum("sprj,pcslj->spclr", legendre, folded, preferred_element_type=jnp.float32)
    return jnp.where(is_valid, result, jnp.zeros_like(result))


def solution(mesh):
    rows = mesh.shape["lat"]

    def local(spectral_in, legendre, wave_of_slot):
        slots, _, _, slabs, _ = spectral_in.shape
        whole_tiles = slots % SLOTS_PER_STEP == 0 and legendre.shape[3] == sum(FORWARD) * LANES
        if rows * FIELDS == 2 * slabs and whole_tiles and wave_of_slot.shape[0] % SBLOCK == 0:
            return per_device(spectral_in, legendre, wave_of_slot)
        return per_device_general(spectral_in, legendre, wave_of_slot)

    return jax.shard_map(
        local,
        mesh=mesh,
        in_specs=(P("lat", None, None, "ens", None), P("lat", None, None, None), P()),
        out_specs=P("lat", None, None, "ens", None),
        check_vma=False,
    )
```

```python
import math

import jax
import jax.numpy as jnp
from jax import lax
from jax.experimental import pallas as pl
from jax.experimental.pallas import tpu as pltpu
from jax.sharding import PartitionSpec as P

NLON = 2560
FIELDS = 4
HALF = NLON // 2
LANES = 128
SLOTS_PER_STEP = 20
XBLOCK = 256
SBLOCK = 128
VMEM = 56 << 20
FORWARD = (1, 4)
RETURN = ((0, 0, 1), (1, 0, 3), (1, 3, 1))


def quarter_sine(t):
    u = t * t
    p = jnp.float32(-3.5988432e-6)
    for coefficient in (1.60441184787e-4, -4.68175413532e-3, 7.96926262462e-2, -6.45964097506e-1, 1.57079632679):
        p = p * u + jnp.float32(coefficient)
    return p * t


def phase_turn(waves, points):
    product = waves * points
    return product - NLON * jnp.round(product * (1.0 / NLON))


def cosine_of(turn):
    return quarter_sine((HALF // 2 - jnp.abs(turn)) * (2.0 / HALF))


def sine_of(turn):
    size = jnp.abs(turn)
    return jnp.sign(turn) * quarter_sine(jnp.minimum(size, HALF - size) * (2.0 / HALF))


def half_tables(waves):
    m = waves.astype(jnp.float32)
    factor = 1.0 / math.sqrt(NLON)
    weight = jnp.where(waves == 0, 1.0, 2.0).astype(jnp.float32)
    x = jnp.arange(HALF + 16, dtype=jnp.float32)
    turn = phase_turn(m[None, :], x[:, None])
    synthesis_cos = (cosine_of(turn) * factor * weight[None, :]).astype(jnp.bfloat16)
    synthesis_sin = (-sine_of(turn[:HALF]) * factor * weight[None, :]).astype(jnp.bfloat16)
    x = x[:HALF]
    twice = jnp.where(x == 0, 1.0, 2.0)[None, :]
    turn = phase_turn(m[:, None], x[None, :])
    analysis_cos = (cosine_of(turn) * factor * twice).astype(jnp.bfloat16)
    analysis_sin = (-sine_of(turn) * factor * twice).astype(jnp.bfloat16)
    alternate = jnp.where(waves % 2 == 0, factor, -factor).astype(jnp.bfloat16).astype(jnp.float32)
    return synthesis_cos, synthesis_sin, analysis_cos, analysis_sin, alternate[:, None]


def synthesis_kernel(count_ref, spectral_ref, legendre_ref, out_ref, scratch):
    step = pl.program_id(1)
    levels = out_ref.shape[0] // 2
    rows = spectral_ref.shape[2] * spectral_ref.shape[3]
    half = spectral_ref.shape[4]
    lane = lax.broadcasted_iota(jnp.int32, (rows, half), 1)
    for s in range(SLOTS_PER_STEP):
        parts = []
        for p in range(2):
            values = spectral_ref[s, p].reshape(rows, half).astype(jnp.float32)
            count = count_ref[step * SLOTS_PER_STEP + s, p]
            values = jnp.where(lane < count, values, 0.0).astype(jnp.bfloat16)
            parts.append(jnp.dot(values, legendre_ref[s, p], preferred_element_type=jnp.float32))
        scratch[s, 0] = parts[0] + parts[1]
        scratch[s, 1] = parts[0] - parts[1]
        for v in range(levels):
            for ns in range(2):
                tile = scratch[s, ns, pl.ds(v, rows // levels, stride=levels), :]
                out_ref[2 * v + ns, 0, s] = tile.astype(jnp.bfloat16)


def synthesize(counts, spectral, legendre, units):
    slots, _, _, slabs, half = spectral.shape
    levels = slabs // FIELDS
    rows = 2 * FIELDS
    return pl.pallas_call(
        synthesis_kernel,
        grid_spec=pltpu.PrefetchScalarGridSpec(
            num_scalar_prefetch=1,
            grid=(len(units), slots // SLOTS_PER_STEP),
            in_specs=[
                pl.BlockSpec((SLOTS_PER_STEP, 2, 2, slabs, half), lambda u, i, c: (i, 0, 0, 0, 0)),
                pl.BlockSpec((SLOTS_PER_STEP, 2, half, LANES), lambda u, i, c: (i, 0, 0, units[0] + u)),
            ],
            out_specs=pl.BlockSpec((2 * levels, 1, SLOTS_PER_STEP, rows, LANES), lambda u, i, c: (0, u, i, 0, 0)),
            scratch_shapes=[pltpu.VMEM((SLOTS_PER_STEP, 2, 2 * slabs, LANES), jnp.float32)],
        ),
        out_shape=jax.ShapeDtypeStruct((2 * levels, len(units), slots, rows, LANES), jnp.bfloat16),
        compiler_params=pltpu.CompilerParams(vmem_limit_bytes=VMEM),
        cost_estimate=pl.CostEstimate(
            flops=2 * slots * 2 * 2 * slabs * half * LANES,
            transcendentals=0,
            bytes_accessed=slots * 2 * half * (LANES + 2 * slabs) * 2,
        ),
        name="legendre_synthesis",
    )(counts, spectral, legendre)


def grid_kernel(y_ref, sc_ref, ss_ref, ac_ref, as_ref, alt_ref, out_ref, wide, cos_in, sin_in, even, odd):
    ranks, _, slots, rows, _ = y_ref.shape
    waves = ranks * slots
    wide[...] = y_ref[...].reshape(waves * rows, LANES).astype(jnp.float32)
    for f in range(FIELDS):
        columns = pl.ds(f * LANES, LANES)
        cos_in[:, columns] = wide[pl.ds(f, waves, stride=rows), :].astype(jnp.bfloat16)
        sin_in[:, columns] = wide[pl.ds(FIELDS + f, waves, stride=rows), :].astype(jnp.bfloat16)

    def partner(a):
        return jnp.concatenate([a[:, LANES:], a[:, :LANES]], axis=1)

    for b in range(HALF // XBLOCK):
        points = pl.ds(b * XBLOCK, XBLOCK)
        e = jnp.dot(sc_ref[points, :], cos_in[...], preferred_element_type=jnp.float32)
        o = jnp.dot(ss_ref[points, :], sin_in[...], preferred_element_type=jnp.float32)
        e2, o2 = partner(e), partner(o)
        even[points, :] = (e * e2 + o * o2).astype(jnp.bfloat16)
        odd[points, :] = (e * o2 + o * e2).astype(jnp.bfloat16)
    middle = jnp.dot(sc_ref[pl.ds(HALF, 16), :], cos_in[...], preferred_element_type=jnp.float32)
    middle = (middle * partner(middle)).astype(jnp.bfloat16).astype(jnp.float32)[0:1, :]

    for b in range(waves // SBLOCK):
        part = pl.ds(b * SBLOCK, SBLOCK)
        cos_out = jnp.dot(ac_ref[part, :], even[...], preferred_element_type=jnp.float32)
        cos_out = cos_out + alt_ref[part, :] * middle
        sin_out = jnp.dot(as_ref[part, :], odd[...], preferred_element_type=jnp.float32)
        for f in range(FIELDS):
            columns = slice(f * LANES, (f + 1) * LANES)
            wide[pl.ds(b * SBLOCK * rows + f, SBLOCK, stride=rows), :] = cos_out[:, columns]
            wide[pl.ds(b * SBLOCK * rows + FIELDS + f, SBLOCK, stride=rows), :] = sin_out[:, columns]
    out_ref[...] = wide[...].astype(jnp.bfloat16).reshape(ranks, 1, slots, rows, LANES)


def grid_product(y, tables, first, units):
    ranks, _, slots, rows, _ = y.shape
    waves = ranks * slots
    width = FIELDS * LANES
    return pl.pallas_call(
        grid_kernel,
        grid=(units,),
        in_specs=[pl.BlockSpec((ranks, 1, slots, rows, LANES), lambda u: (0, first + u, 0, 0, 0))]
        + [pl.BlockSpec(t.shape, lambda u: (0, 0)) for t in tables],
        out_specs=pl.BlockSpec((ranks, 1, slots, rows, LANES), lambda u: (0, u, 0, 0, 0)),
        out_shape=jax.ShapeDtypeStruct((ranks, units, slots, rows, LANES), jnp.bfloat16),
        scratch_shapes=[
            pltpu.VMEM((waves * rows, LANES), jnp.float32),
            pltpu.VMEM((waves, width), jnp.bfloat16),
            pltpu.VMEM((waves, width), jnp.bfloat16),
            pltpu.VMEM((HALF, width), jnp.bfloat16),
            pltpu.VMEM((HALF, width), jnp.bfloat16),
        ],
        compiler_params=pltpu.CompilerParams(vmem_limit_bytes=VMEM),
        cost_estimate=pl.CostEstimate(
            flops=units * 8 * waves * HALF * width,
            transcendentals=0,
            bytes_accessed=8 * waves * HALF + units * 4 * waves * rows * LANES,
        ),
        name="grid_product",
    )(y, *tables)


def projection_kernel(sizes, added, count_ref, *refs):
    chunks = sum(sizes)
    arrived = refs[: len(sizes)]
    legendres = refs[len(sizes) : len(sizes) + chunks]
    before = refs[len(sizes) + chunks] if added else None
    homes = [(arrived[c], u) for c in range(len(sizes)) for u in range(sizes[c])]
    out_ref, scratch = refs[-2], refs[-1]
    step = pl.program_id(0)
    levels = arrived[0].shape[0] // 2
    fields = arrived[0].shape[3]
    rows = levels * fields
    half = legendres[0].shape[2]
    lane = lax.broadcasted_iota(jnp.int32, (rows, half), 1)
    for s in range(SLOTS_PER_STEP):
        sums = [None, None]
        for k in range(chunks):
            for v in range(levels):
                ref, u = homes[k]
                north = ref[2 * v, u, s].astype(jnp.float32)
                south = ref[2 * v + 1, u, s].astype(jnp.float32)
                scratch[s, k, 0, pl.ds(v * fields, fields), :] = north + south
                scratch[s, k, 1, pl.ds(v * fields, fields), :] = north - south
            for p in range(2):
                folded = jnp.concatenate(
                    [scratch[s, k, p, pl.ds(r, levels, stride=fields), :] for r in range(fields)], axis=0
                ).astype(jnp.bfloat16)
                part = lax.dot_general(
                    folded, legendres[k][s, p], (((1,), (1,)), ((), ())), preferred_element_type=jnp.float32
                )
                sums[p] = part if sums[p] is None else sums[p] + part
        for p in range(2):
            count = count_ref[step * SLOTS_PER_STEP + s, p]
            value = jnp.where(lane < count, sums[p], 0.0).reshape(out_ref.shape[2:])
            if added:
                value = value + before[s, p]
            out_ref[s, p] = value


def project(counts, arrived, legendre, chunk_ids, before=None):
    sizes = [a.shape[1] for a in arrived]
    chunks = len(chunk_ids)
    ranks, _, slots, fields, _ = arrived[0].shape
    slabs = ranks // 2 * FIELDS
    half = legendre.shape[2]
    n = SLOTS_PER_STEP
    out_spec = pl.BlockSpec((n, 2, 2, slabs, half), lambda i, c: (i, 0, 0, 0, 0))
    added = before is not None

    def kernel(*refs):
        projection_kernel(sizes, added, *refs)

    return pl.pallas_call(
        kernel,
        grid_spec=pltpu.PrefetchScalarGridSpec(
            num_scalar_prefetch=1,
            grid=(slots // n,),
            in_specs=[pl.BlockSpec((ranks, size, n, fields, LANES), lambda i, c: (0, 0, i, 0, 0)) for size in sizes]
            + [pl.BlockSpec((n, 2, half, LANES), lambda i, c, k=k: (i, 0, 0, k)) for k in chunk_ids]
            + ([out_spec] if added else []),
            out_specs=out_spec,
            scratch_shapes=[pltpu.VMEM((n, chunks, 2, 2 * slabs, LANES), jnp.float32)],
        ),
        out_shape=jax.ShapeDtypeStruct((slots, 2, 2, slabs, half), jnp.float32),
        input_output_aliases={1 + len(sizes) + chunks: 0} if added else {},
        compiler_params=pltpu.CompilerParams(vmem_limit_bytes=VMEM),
        cost_estimate=pl.CostEstimate(
            flops=2 * chunks * slots * 2 * 2 * slabs * half * LANES,
            transcendentals=0,
            bytes_accessed=slots * 2 * half * (chunks * LANES + 4 * slabs) * 2,
        ),
        name="legendre_projection",
    )(counts, *arrived, *([legendre] * chunks), *([before] if added else []))


def per_device(spectral_in, legendre, wave_of_slot):
    slots, _, _, slabs, half = spectral_in.shape
    total = wave_of_slot.shape[0]
    ranks = total // slots
    start = lax.axis_index("lat") * slots
    own = lax.dynamic_slice_in_dim(wave_of_slot, start, slots)
    counts = (total + 1 - own[:, None] - jnp.arange(2, dtype=jnp.int32)[None, :]) // 2
    tables = half_tables(wave_of_slot)

    def exchange(x):
        return lax.all_to_all(x, "lat", split_axis=0, concat_axis=0, tiled=True)

    sent, at = [], 0
    for size in FORWARD:
        sent.append(exchange(synthesize(counts, spectral_in, legendre, range(at, at + size))))
        at += size
    back = [exchange(grid_product(sent[c], tables, first, units)) for c, first, units in RETURN]
    places = [sum(FORWARD[:c]) + first for c, first, _ in RETURN]
    ids = [list(range(p, p + r[2])) for p, r in zip(places, RETURN)]
    sums = project(counts, back[:-1], legendre, [k for i in ids[:-1] for k in i])
    return project(counts, back[-1:], legendre, ids[-1], sums)


def basis_tables(wave_of_slot):
    longitudes = jnp.arange(NLON, dtype=jnp.int32)
    phases = wave_of_slot[:, None] * longitudes[None, :] % NLON
    angles = phases.astype(jnp.float32) * (2.0 * math.pi / NLON)
    factor = 1.0 / math.sqrt(NLON)
    cosine = jnp.cos(angles) * factor
    sine_part = jnp.sin(angles) * factor
    weights = jnp.where(wave_of_slot == 0, 1.0, 2.0).astype(jnp.float32)[:, None]
    synthesis = jnp.stack([weights * cosine, -weights * sine_part]).astype(jnp.bfloat16)
    analysis = jnp.stack([cosine, -sine_part]).astype(jnp.bfloat16)
    return synthesis, analysis


def per_device_general(spectral_in, legendre, wave_of_slot):
    slot_count, _, half, north = legendre.shape
    total = wave_of_slot.shape[0]
    own = lax.dynamic_slice_in_dim(wave_of_slot, lax.axis_index("lat") * slot_count, slot_count)
    ranks = 2 * jnp.arange(half, dtype=jnp.int32)[None, :] + jnp.arange(2, dtype=jnp.int32)[:, None]
    is_valid = (ranks[None] <= (total - 1 - own)[:, None, None])[:, :, None, None, :]
    masked = jnp.where(is_valid, spectral_in, jnp.zeros_like(spectral_in))
    sums = jnp.einsum("sprj,spclr->spclj", legendre, masked, preferred_element_type=jnp.float32)
    south = (sums[:, 0] - sums[:, 1])[..., ::-1]
    fourier = jnp.concatenate([sums[:, 0] + sums[:, 1], south], axis=3).astype(jnp.bfloat16)
    spread = lax.all_to_all(fourier, "lat", split_axis=3, concat_axis=0, tiled=True)
    synthesis, analysis = basis_tables(wave_of_slot)
    field = jnp.einsum("scli,csx->lix", spread, synthesis, preferred_element_type=jnp.float32)
    levels = field.shape[0] // FIELDS
    partner = jnp.roll(field.reshape((FIELDS, levels) + field.shape[1:]), -1, axis=0).reshape(field.shape)
    product = (field * partner).astype(jnp.bfloat16)
    coefficients = jnp.einsum("lix,csx->csli", product, analysis, preferred_element_type=jnp.float32)
    gathered = lax.all_to_all(coefficients.astype(jnp.bfloat16), "lat", split_axis=1, concat_axis=3, tiled=True)
    north_part = gathered[..., :north].astype(jnp.float32)
    south_part = gathered[..., north:][..., ::-1].astype(jnp.float32)
    folded = jnp.stack([north_part + south_part, north_part - south_part]).astype(jnp.bfloat16)
    result = jnp.einsum("sprj,pcslj->spclr", legendre, folded, preferred_element_type=jnp.float32)
    return jnp.where(is_valid, result, jnp.zeros_like(result))


def solution(mesh):
    rows = mesh.shape["lat"]

    def local(spectral_in, legendre, wave_of_slot):
        slots, _, _, slabs, _ = spectral_in.shape
        whole_tiles = slots % SLOTS_PER_STEP == 0 and legendre.shape[3] == sum(FORWARD) * LANES
        if rows * FIELDS == 2 * slabs and whole_tiles and wave_of_slot.shape[0] % SBLOCK == 0:
            return per_device(spectral_in, legendre, wave_of_slot)
        return per_device_general(spectral_in, legendre, wave_of_slot)

    return jax.shard_map(
        local,
        mesh=mesh,
        in_specs=(P("lat", None, None, "ens", None), P("lat", None, None, None), P()),
        out_specs=P("lat", None, None, "ens", None),
        check_vma=False,
    )
```
